256 devices in a mesh: layer: 4 (over y_hi, core), feat: 64 (over y_lo, z, x).
Axes of the slice: x: 4, y: 4 (y_hi: 2, y_lo: 2; y = y_hi * 2 + y_lo), z: 8, core: 2. Of those that a mesh axis runs over, the one named last changes fastest.
Arguments:
- inputs: bfloat16 [768, 4, 2048], P('feat', 'layer'), may hold values from -6 to 6
- w_enc: bfloat16 [4, 2048, 16384], P('layer', None, 'feat'), may hold values from -6 to 6
- b_enc: bfloat16 [16384], P('feat'), may hold values from -3 to 3
- w_dec: bfloat16 [16384, 4, 2048], P('feat', 'layer'), may hold values from -15 to 15
- b_dec: bfloat16 [4, 2048], P('layer'), may hold values from -3 to 3
Outputs:
- recon: bfloat16 [768, 4, 2048], P('feat', 'layer')
- new_enc: float32 [4, 2048, 16384], P('layer', None, 'feat')
- new_dec: float32 [16384, 4, 2048], P('feat', 'layer')
The draws below stay inside these ranges and needn't reach their ends.
All inputs are finite; a program needn't handle non-finite values.
Results may differ from the reference program's by a relative error of at most 0.0055.
Values may be sent and summed in bfloat16 or wider, within the bound.
No kernel may reach another device: no remote copies, remote signals or barrier semaphores. Data moves between devices by JAX's collectives and lax.ppermute only.
A program may use at most 64 MiB of HBM per device.

```python
import math
import jax
import jax.numpy as jnp
from jax import lax

D = 2048
F = 16384
L = 4
TOKENS = 768


def draw_w_dec(key, part):
    entry_key, row_key = jax.random.split(jax.random.fold_in(key, 11))
    layer_scale = 0.6 + 1.2 * jnp.arange(L, dtype=jnp.float32) / max(L - 1, 1)
    entries = jax.random.truncated_normal(entry_key, -4.0, 4.0, (F, L, D), jnp.float32)
    row_scale = jnp.exp(jax.random.uniform(row_key, (F,), jnp.float32, math.log(0.2), math.log(2.0)))
    return (entries * row_scale[:, None, None] * layer_scale[None, :, None]).astype(jnp.bfloat16)


def levels(stream_key, extent, pieces, least, top_value):
    loudness, own = 1.0, jax.random.fold_in(stream_key, 6)
    for dim, blocks in pieces:
        steps = jnp.exp(jax.random.uniform(jax.random.fold_in(own, dim), (blocks,), jnp.float32, least / len(pieces), top_value / len(pieces)))
        loudness = loudness * jnp.repeat(steps, extent[dim] // blocks).reshape([-1 if axis == dim else 1 for axis in range(len(extent))])
    return loudness


def gaussian(rng, extent, spread, most, pieces=(), held_as=jnp.bfloat16):
    array = spread * jax.random.normal(rng, extent, jnp.float32)
    if pieces:
        array = array * levels(rng, extent, pieces, -0.22, 0.18)
    return jnp.clip(array, -most, most).astype(held_as)


def setup_inputs(seed: int = 0) -> dict:
    keys = jax.random.split(jax.random.key(seed), 6)
    inputs = gaussian(keys[0], (TOKENS, L, D), 1.0, 6.0, ((0, 64), (1, 4)))
    w_enc = gaussian(keys[1], (L, D, F), 1.0, 6.0, ((0, 4), (2, 64)))
    b_enc = gaussian(keys[2], (F,), 0.5, 3.0, ((0, 64),))
    w_dec = draw_w_dec(jax.random.fold_in(keys[5], 71), 0)
    b_dec = gaussian(keys[4], (L, D), 0.5, 3.0, ((0, 4),))
    return {"inputs": inputs, "w_enc": w_enc, "b_enc": b_enc, "w_dec": w_dec, "b_dec": b_dec}


LEARN_RATE = 1.0
SHRINK_LEVEL = 0.5
EPSILON = 1e-06

def reference(inputs, w_enc, b_enc, w_dec, b_dec):
    scale_enc = 1.0 / math.sqrt(L * D)
    scale_dec = 1.0 / math.sqrt(F)
    x_flat = inputs.reshape(TOKENS, L * D)
    enc_mat = w_enc.reshape(L * D, F)
    dec_mat = w_dec.reshape(F, L * D)
    pre_act = jnp.dot(x_flat, enc_mat, preferred_element_type=jnp.float32) * scale_enc + b_enc.astype(jnp.float32)
    latent = jnp.maximum(pre_act, 0.0).astype(jnp.bfloat16)
    recon_full = jnp.dot(latent, dec_mat, preferred_element_type=jnp.float32) * scale_dec + b_dec.reshape(L * D).astype(jnp.float32)
    recon = recon_full.astype(jnp.bfloat16).reshape(TOKENS, L, D)
    errors = (recon_full - x_flat.astype(jnp.float32)).astype(jnp.bfloat16)
    grad_latent = lax.dot_general(errors, dec_mat, (((1,), (1,)), ((), ())), preferred_element_type=jnp.float32) * scale_dec
    grad_pre = jnp.where(pre_act > 0.0, grad_latent, 0.0).astype(jnp.bfloat16)
    grad_enc = lax.dot_general(x_flat, grad_pre, (((0,), (0,)), ((), ())), preferred_element_type=jnp.float32) * scale_enc
    new_enc = (enc_mat.astype(jnp.float32) - LEARN_RATE * grad_enc).reshape(L, D, F)
    grad_dec = lax.dot_general(latent, errors, (((0,), (0,)), ((), ())), preferred_element_type=jnp.float32) * scale_dec
    half_dec = dec_mat.astype(jnp.float32) - LEARN_RATE * grad_dec
    row_rms = jnp.sqrt(lax.optimization_barrier(jnp.sum(half_dec * half_dec, axis=1)) / (L * D) + EPSILON)
    factor = jnp.maximum(0.0, 1.0 - SHRINK_LEVEL / row_rms)
    new_dec = (half_dec * factor[:, None]).reshape(F, L, D)
    return (recon, new_enc, new_dec)
```

```python
import math

import jax
import jax.numpy as jnp
from jax import lax
from jax.sharding import Mesh, PartitionSpec as P

D = 2048
F = 16384
L = 4
SIZES = {"yh": 2, "core": 2, "yl": 2, "z": 8, "x": 4}
LEARN_RATE = 1.0
SHRINK_LEVEL = 0.5
EPSILON = 1e-06
f32 = jnp.float32
bf16 = jnp.bfloat16


def shift(a, axis, k):
    n = SIZES[axis]
    return lax.ppermute(a, axis, [(i, (i + k) % n) for i in range(n)])


def gather_tokens(own):
    pair = jnp.concatenate([own, shift(own, "yl", 1)], axis=0)
    plane = jnp.concatenate([pair, shift(pair, "x", 1), shift(pair, "x", -1), shift(pair, "x", 2)], axis=0)
    half = plane.shape[1] // 2
    down, up = [plane], [plane]
    for _ in range(3):
        down.append(shift(down[-1], "z", 1))
        up.append(shift(up[-1], "z", -1))
    far = jnp.concatenate([shift(down[-1][:, :half], "z", 1), shift(up[-1][:, half:], "z", -1)], axis=1)
    return [plane, down[1], up[1], down[2], up[2], down[3], up[3], far]


def scatter_tokens(blocks):
    home, down1, up1, down2, up2, down3, up3, far = blocks
    half = far.shape[1] // 2
    got = shift(far[:, :half].astype(bf16), "z", -1).astype(f32)
    low = down3 + jnp.pad(got, ((0, 0), (0, half)))
    got = shift(far[:, half:].astype(bf16), "z", 1).astype(f32)
    high = up3 + jnp.pad(got, ((0, 0), (half, 0)))
    for down, up in ((down2, up2), (down1, up1), (home, 0.0)):
        low = down + shift(low.astype(bf16), "z", -1).astype(f32)
        high = up + shift(high.astype(bf16), "z", 1).astype(f32)
    plane = low + high
    rows = plane.shape[0] // 4
    pair = plane[:rows]
    for i, k in ((1, -1), (2, 1), (3, 2)):
        pair = pair + shift(plane[i * rows:(i + 1) * rows].astype(bf16), "x", k).astype(f32)
    rows //= 2
    return pair[:rows] + shift(pair[rows:].astype(bf16), "yl", 1).astype(f32)


def body(inputs, w_enc, b_enc, w_dec, b_dec):
    rows = inputs.shape[0]
    nf = w_enc.shape[2]
    scale_enc = 1.0 / math.sqrt(L * D)
    scale_dec = 1.0 / math.sqrt(F)
    x = inputs.reshape(rows, D)
    enc = w_enc.reshape(D, nf)
    dec = w_dec.reshape(nf, D)
    core = lax.axis_index("core")
    x_all = jnp.concatenate(gather_tokens(x), axis=0)
    tokens = x_all.shape[0]
    half = tokens // 2

    def core_sum(part, kind):
        keep = lax.dynamic_slice_in_dim(part, core * half, half, 0)
        send = lax.dynamic_slice_in_dim(part, (1 - core) * half, half, 0)
        return keep + shift(send.astype(kind), "core", 1).astype(f32)

    def core_join(part):
        other = shift(part, "core", 1)
        return jnp.where(core == 0, jnp.concatenate([part, other], 0), jnp.concatenate([other, part], 0))

    part = core_sum(jnp.dot(x_all, enc, preferred_element_type=f32), f32)
    pre = (part + shift(part, "yh", 1)) * scale_enc + b_enc.astype(f32)
    latent = core_join(jnp.maximum(pre, 0.0).astype(bf16))
    recon_part = jnp.dot(latent, dec, preferred_element_type=f32)
    block = tokens // 8
    summed = scatter_tokens([recon_part[i * block:(i + 1) * block] for i in range(8)])
    recon_local = summed * scale_dec + b_dec.reshape(D).astype(f32)
    err = (recon_local - x.astype(f32)).astype(bf16)
    err_all = jnp.concatenate(gather_tokens(err), axis=0)
    recon = recon_local.astype(bf16).reshape(rows, 1, D)
    grad_dec = lax.dot_general(latent, err_all, (((0,), (0,)), ((), ())), preferred_element_type=f32) * scale_dec
    half_dec = dec.astype(f32) - LEARN_RATE * grad_dec
    square = jnp.sum(half_dec * half_dec, axis=1)
    square = square + shift(square, "core", 1)
    square = square + shift(square, "yh", 1)
    grad_part = lax.dot_general(err_all, dec, (((1,), (1,)), ((), ())), preferred_element_type=f32)
    grad_part = core_sum(grad_part, bf16)
    grad = (grad_part + shift(grad_part.astype(bf16), "yh", 1).astype(f32)) * scale_dec
    grad_pre = core_join(jnp.where(pre > 0.0, grad, 0.0).astype(bf16))
    grad_enc = lax.dot_general(x_all, grad_pre, (((0,), (0,)), ((), ())), preferred_element_type=f32) * scale_enc
    new_enc = (enc.astype(f32) - LEARN_RATE * grad_enc).reshape(1, D, nf)
    row_rms = jnp.sqrt(square / (L * D) + EPSILON)
    factor = jnp.maximum(0.0, 1.0 - SHRINK_LEVEL / row_rms)
    new_dec = (half_dec * factor[:, None]).reshape(nf, 1, D)
    return recon, new_enc, new_dec


def solution(mesh):
    fine = Mesh(mesh.devices.reshape(2, 2, 2, 8, 4), ("yh", "core", "yl", "z", "x"))
    layer, feat = ("yh", "core"), ("yl", "z", "x")
    return jax.shard_map(
        body,
        mesh=fine,
        in_specs=(P(feat, layer, None), P(layer, None, feat), P(feat), P(feat, layer, None), P(layer, None)),
        out_specs=(P(feat, layer, None), P(layer, None, feat), P(feat, layer, None)),
        check_vma=False,
    )
```

```python
import functools
import math

import jax
import jax.numpy as jnp
from jax import lax
from jax.experimental import pallas as pl
from jax.experimental.pallas import tpu as pltpu
from jax.sharding import Mesh, PartitionSpec as P

D = 2048
F = 16384
L = 4
SIZES = {"yh": 2, "core": 2, "yl": 2, "z": 8, "x": 4}
LEARN_RATE = 1.0
SHRINK_LEVEL = 0.5
EPSILON = 1e-06
STREAMS = 2
f32 = jnp.float32
bf16 = jnp.bfloat16


def shift(a, axis, k):
    n = SIZES[axis]
    return lax.ppermute(a, axis, [(i, (i + k) % n) for i in range(n)])


def gather_tokens(own):
    pair = jnp.concatenate([own, shift(own, "yl", 1)], axis=0)
    plane = jnp.concatenate([pair, shift(pair, "x", 1), shift(pair, "x", -1), shift(pair, "x", 2)], axis=0)
    half = plane.shape[1] // 2
    pieces, down, up = [(plane, 0, 0)], plane, plane
    for i in range(3):
        down, up = shift(down, "z", 1), shift(up, "z", -1)
        pieces += [(down, 2 * i + 1, 0), (up, 2 * i + 2, 0)]
    pieces += [(shift(down[:, :half], "z", 1), 7, 0), (shift(up[:, half:], "z", -1), 7, half)]
    return pieces


def gather_streams(own):
    width = own.shape[1] // STREAMS
    pieces = []
    for s in range(STREAMS):
        for piece, block, col in gather_tokens(own[:, s * width:(s + 1) * width]):
            pieces.append((piece, block * piece.shape[0], col + s * width))
    return [p[0] for p in pieces], tuple((p[1], p[2]) for p in pieces)


def scatter_tokens(blocks):
    home, down1, up1, down2, up2, down3, up3, far = blocks
    half = far.shape[1] // 2
    got = shift(far[:, :half].astype(bf16), "z", -1).astype(f32)
    low = down3 + jnp.pad(got, ((0, 0), (0, half)))
    got = shift(far[:, half:].astype(bf16), "z", 1).astype(f32)
    high = up3 + jnp.pad(got, ((0, 0), (half, 0)))
    for down, up in ((down2, up2), (down1, up1), (home, 0.0)):
        low = down + shift(low.astype(bf16), "z", -1).astype(f32)
        high = up + shift(high.astype(bf16), "z", 1).astype(f32)
    plane = low + high
    rows = plane.shape[0] // 4
    pair = plane[:rows]
    for i, k in ((1, -1), (2, 1), (3, 2)):
        pair = pair + shift(plane[i * rows:(i + 1) * rows].astype(bf16), "x", k).astype(f32)
    rows //= 2
    return pair[:rows] + shift(pair[rows:].astype(bf16), "yl", 1).astype(f32)


def place(all_ref, refs, places):
    for ref, (row, col) in zip(refs, places):
        h, w = ref.shape
        all_ref[row:row + h, col:col + w] = ref[...]


def pre_kernel(places, core_ref, enc_ref, *refs):
    *pieces, x_all, keep, send, part = refs
    place(x_all, pieces, places)
    part[...] = jnp.dot(x_all[...], enc_ref[...], preferred_element_type=f32)
    core, half = core_ref[0], keep.shape[0]
    keep[...] = part[pl.ds(pl.multiple_of(core * half, half), half), :]
    send[...] = part[pl.ds(pl.multiple_of((1 - core) * half, half), half), :]


def grad_kernel(places, core_ref, latent_ref, dec_ref, *refs):
    *pieces, keep, send, half_dec, square, err_all, part = refs
    place(err_all, pieces, places)
    part[...] = lax.dot_general(err_all[...], dec_ref[...], (((1,), (1,)), ((), ())), preferred_element_type=f32)
    core, half = core_ref[0], keep.shape[0]
    keep[...] = part[pl.ds(pl.multiple_of(core * half, half), half), :]
    send[...] = part[pl.ds(pl.multiple_of((1 - core) * half, half), half), :].astype(bf16)
    scale = LEARN_RATE / math.sqrt(F)
    grad = lax.dot_general(latent_ref[...], err_all[...], (((0,), (0,)), ((), ())), preferred_element_type=f32)
    half_dec[...] = dec_ref[...].astype(f32) - grad * scale
    square[...] = jnp.sum(half_dec[...] * half_dec[...], axis=1, keepdims=True)


def call(kernel, outs, scratch, smem, *args):
    vmem = pl.BlockSpec(memory_space=pltpu.VMEM)
    return pl.pallas_call(
        kernel,
        out_shape=[jax.ShapeDtypeStruct(s, d) for s, d in outs],
        in_specs=[pl.BlockSpec(memory_space=pltpu.SMEM)] + [vmem] * len(args),
        out_specs=[vmem] * len(outs),
        scratch_shapes=[pltpu.VMEM(s, d) for s, d in scratch],
        compiler_params=pltpu.CompilerParams(vmem_limit_bytes=48 * 1024 * 1024),
    )(smem, *args)


def body(inputs, w_enc, b_enc, w_dec, b_dec):
    rows = inputs.shape[0]
    nf = w_enc.shape[2]
    tokens = rows * 64
    half = tokens // 2
    scale_enc = 1.0 / math.sqrt(L * D)
    scale_dec = 1.0 / math.sqrt(F)
    x = inputs.reshape(rows, D)
    enc = w_enc.reshape(D, nf)
    dec = w_dec.reshape(nf, D)
    core = lax.axis_index("core")
    core_arr = core.reshape(1)

    def core_join(part):
        other = shift(part, "core", 1)
        return jnp.where(core == 0, jnp.concatenate([part, other], 0), jnp.concatenate([other, part], 0))

    pieces, places = gather_streams(x)
    x_all, keep, send = call(
        functools.partial(pre_kernel, places),
        [((tokens, D), bf16), ((half, nf), f32), ((half, nf), f32)],
        [((tokens, nf), f32)],
        core_arr, enc, *pieces)
    part = keep + shift(send, "core", 1)
    pre = (part + shift(part, "yh", 1)) * scale_enc + b_enc.astype(f32)
    latent = core_join(jnp.maximum(pre, 0.0).astype(bf16))
    block = tokens // 8
    width = D // STREAMS
    recons, errs = [], []
    bias = b_dec.reshape(D).astype(f32)
    gathered, err_places = [], []
    for s in range(STREAMS):
        cols = slice(s * width, (s + 1) * width)
        recon_part = jnp.dot(latent, dec[:, cols], preferred_element_type=f32)
        summed = scatter_tokens([recon_part[i * block:(i + 1) * block] for i in range(8)])
        recon_local = summed * scale_dec + bias[cols]
        err = (recon_local - x[:, cols].astype(f32)).astype(bf16)
        recons.append(recon_local.astype(bf16))
        for piece, b, col in gather_tokens(err):
            gathered.append(piece)
            err_places.append((b * block, col + s * width))
    recon = jnp.concatenate(recons, axis=1).reshape(rows, 1, D)
    keep, send, half_dec, square = call(
        functools.partial(grad_kernel, tuple(err_places)),
        [((half, nf), f32), ((half, nf), bf16), ((nf, D), f32), ((nf, 1), f32)],
        [((tokens, D), bf16), ((tokens, nf), f32)],
        core_arr, latent, dec, *gathered)
    grad_part = keep + shift(send, "core", 1).astype(f32)
    square = square.reshape(nf)
    square = square + shift(square, "core", 1)
    square = square + shift(square, "yh", 1)
    grad = (grad_part + shift(grad_part.astype(bf16), "yh", 1).astype(f32)) * scale_dec
    grad_pre = core_join(jnp.where(pre > 0.0, grad, 0.0).astype(bf16))
    grad_enc = lax.dot_general(x_all, grad_pre, (((0,), (0,)), ((), ())), preferred_element_type=f32) * scale_enc
    new_enc = (enc.astype(f32) - LEARN_RATE * grad_enc).reshape(1, D, nf)
    row_rms = jnp.sqrt(square / (L * D) + EPSILON)
    factor = jnp.maximum(0.0, 1.0 - SHRINK_LEVEL / row_rms)
    new_dec = (half_dec * factor[:, None]).reshape(nf, 1, D)
    return recon, new_enc, new_dec


def solution(mesh):
    fine = Mesh(mesh.devices.reshape(2, 2, 2, 8, 4), ("yh", "core", "yl", "z", "x"))
    layer, feat = ("yh", "core"), ("yl", "z", "x")
    return jax.shard_map(
        body,
        mesh=fine,
        in_specs=(P(feat, layer, None), P(layer, None, feat), P(feat), P(feat, layer, None), P(layer, None)),
        out_specs=(P(feat, layer, None), P(layer, None, feat), P(feat, layer, None)),
        check_vma=False,
    )
```

```python
import functools
import math

import jax
import jax.numpy as jnp
from jax import lax
from jax.experimental import pallas as pl
from jax.experimental.pallas import tpu as pltpu
from jax.sharding import Mesh, PartitionSpec as P


D = 2048
F = 16384
L = 4
SIZES = {"yh": 2, "core": 2, "yl": 2, "z": 8, "x": 4}
LEARN_RATE = 1.0
SHRINK_LEVEL = 0.5
EPSILON = 1e-06
SCALE_ENC = 1.0 / math.sqrt(L * D)
SCALE_DEC = 1.0 / math.sqrt(F)
LEAST = 2.0**-126
f32 = jnp.float32
bf16 = jnp.bfloat16


def shift(a, axis, k):
    n = SIZES[axis]
    return lax.ppermute(a, axis, [(i, (i + k) % n) for i in range(n)])


def gather_x(own):
    return jnp.concatenate([own, *(shift(own, "x", k) for k in (1, -1, 2))], axis=0)


def gather_z(plane):
    half = plane.shape[1] // 2
    pieces, places = [plane], [(0, 0)]
    down, up = plane, plane
    for i in range(3):
        down, up = shift(down, "z", 1), shift(up, "z", -1)
        pieces += [down, up]
        places += [(2 * i + 1, 0), (2 * i + 2, 0)]
        down, up = lax.optimization_barrier((down, up))
    pieces += [shift(down[:, :half], "z", 1), shift(up[:, half:], "z", -1)]
    places += [(7, 0), (7, half)]
    return pieces, tuple(places)


def scatter_z(blocks, far_low, far_high):
    home, down1, up1, down2, up2, down3, up3 = blocks
    half = far_low.shape[1]
    low, high = shift(far_low, "z", -1), shift(far_high, "z", 1)
    low, high = lax.optimization_barrier((low, high))
    low = jnp.concatenate([down3[:, :half] + low.astype(f32), down3[:, half:]], axis=1)
    high = jnp.concatenate([up3[:, :half], up3[:, half:] + high.astype(f32)], axis=1)
    for down, up in ((down2, up2), (down1, up1), (home, 0.0)):
        low, high = shift(low.astype(bf16), "z", -1), shift(high.astype(bf16), "z", 1)
        low, high = lax.optimization_barrier((low, high))
        low, high = down + low.astype(f32), up + high.astype(f32)
    return low + high


def scatter_x(plane):
    rows = plane.shape[0] // 4
    total = plane[:rows]
    for i, k in ((1, -1), (2, 1), (3, 2)):
        total = total + shift(plane[i * rows:(i + 1) * rows].astype(bf16), "x", k).astype(f32)
    return total


def rows_of(index, size):
    return pl.ds(pl.multiple_of(index * size, size), size)


def pre_kernel(places, core_ref, enc_ref, enc2_ref, *refs):
    *pieces, x_own, keep, send, part = refs
    r = pieces[0].shape[0]
    for ref, (block, col) in zip(pieces, places):
        x_own[block * r:(block + 1) * r, col:col + ref.shape[1]] = ref[...]
    nf = enc_ref.shape[1]
    part[:, :nf] = jnp.dot(x_own[...], enc_ref[...], preferred_element_type=f32)
    part[:, nf:] = jnp.dot(x_own[...], enc2_ref[...], preferred_element_type=f32)
    core, half = core_ref[0], keep.shape[0]
    keep[...] = part[rows_of(core, half), :]
    send[...] = part[rows_of(1 - core, half), :]


def recon_kernel(core_ref, mine_ref, other_ref, dec_ref, dec2_ref, lat_own, lat_pair, recon, far_low, far_high, latent):
    core, half = core_ref[0], mine_ref.shape[0]
    latent[rows_of(core, half), :] = mine_ref[...]
    latent[rows_of(1 - core, half), :] = other_ref[...]
    nf = dec_ref.shape[0]
    lat_own[...] = latent[:, :nf]
    lat_pair[...] = latent[:, nf:]
    recon[...] = jnp.dot(lat_own[...], dec_ref[...], preferred_element_type=f32)
    recon[...] += jnp.dot(lat_pair[...], dec2_ref[...], preferred_element_type=f32)
    r, cols = far_low.shape
    far_low[...] = recon[7 * r:, :cols].astype(bf16)
    far_high[...] = recon[7 * r:, cols:].astype(bf16)


def grad_kernel(places, core_ref, lat_own, lat_in, dec_ref, *refs):
    *pieces, keep, send, lat_keep, half_dec, square, err_all, latent, part = refs
    r = pieces[0].shape[0] // 2
    half = lat_own.shape[0]
    for ref, (block, col) in zip(pieces, places):
        for pair in range(2):
            err_all[pair * half + block * r:pair * half + (block + 1) * r, col:col + ref.shape[1]] = ref[pair * r:(pair + 1) * r, :]
    latent[:half, :] = lat_own[...]
    latent[half:, :] = lat_in[...]
    part[...] = lax.dot_general(err_all[...], dec_ref[...], (((1,), (1,)), ((), ())), preferred_element_type=f32)
    core = core_ref[0]
    keep[...] = part[rows_of(core, half), :]
    send[...] = part[rows_of(1 - core, half), :].astype(bf16)
    lat_keep[...] = latent[rows_of(core, half), :]
    grad = lax.dot_general(latent[...], err_all[...], (((0,), (0,)), ((), ())), preferred_element_type=f32)
    half_dec[...] = dec_ref[...].astype(f32) - grad * (LEARN_RATE * SCALE_DEC)
    square[...] = jnp.sum(half_dec[...] * half_dec[...], axis=1, keepdims=True)


def enc_kernel(core_ref, mine_ref, other_ref, x_own, x_in, enc_ref, new_enc, grad):
    core, half = core_ref[0], mine_ref.shape[0]
    grad[rows_of(core, half), :] = mine_ref[...]
    grad[rows_of(1 - core, half), :] = other_ref[...]
    dims = (((0,), (0,)), ((), ()))
    total = lax.dot_general(x_own[...], grad[:half, :], dims, preferred_element_type=f32)
    total += lax.dot_general(x_in[...], grad[half:, :], dims, preferred_element_type=f32)
    new_enc[...] = enc_ref[...].astype(f32) - total * (LEARN_RATE * SCALE_ENC)


def call(kernel, outs, scratch, mib, smem, *args):
    vmem = pl.BlockSpec(memory_space=pltpu.VMEM)
    return pl.pallas_call(
        kernel,
        out_shape=[jax.ShapeDtypeStruct(s, d) for s, d in outs],
        in_specs=[pl.BlockSpec(memory_space=pltpu.SMEM)] + [vmem] * len(args),
        out_specs=[vmem] * len(outs),
        scratch_shapes=[pltpu.VMEM(s, d) for s, d in scratch],
        compiler_params=pltpu.CompilerParams(vmem_limit_bytes=mib * 1024 * 1024),
    )(smem, *args)


def step(inputs, w_enc, b_enc, w_dec, b_dec):
    rows = inputs.shape[0]
    nf = w_enc.shape[2]
    tokens = rows * 64
    half, quarter, block = tokens // 2, tokens // 4, rows * 4
    x = inputs.reshape(rows, D)
    enc = w_enc.reshape(D, nf)
    dec = w_dec.reshape(nf, D)
    core = lax.axis_index("core").reshape(1)
    enc2, dec2 = shift(enc, "yl", 1), shift(dec, "yl", 1)
    bias = jnp.concatenate([b_enc, shift(b_enc, "yl", 1)]).astype(f32)

    pieces, places = gather_z(gather_x(x))
    x_own, keep, send = call(
        functools.partial(pre_kernel, places),
        [((half, D), bf16), ((quarter, 2 * nf), f32), ((quarter, 2 * nf), f32)],
        [((half, 2 * nf), f32)], 16,
        core, enc, enc2, *pieces)
    part = keep + shift(send, "core", 1)
    pre = (part + shift(part, "yh", 1)) * SCALE_ENC + bias
    latent = jnp.where(pre > 0.0, jnp.maximum(pre, LEAST), 0.0).astype(bf16)
    lat_own, lat_pair, recon_part, far_low, far_high = call(
        recon_kernel,
        [((half, nf), bf16), ((half, nf), bf16), ((half, D), f32), ((block, D // 2), bf16), ((block, D // 2), bf16)],
        [((half, 2 * nf), bf16)], 16,
        core, latent, shift(latent, "core", 1), dec, dec2)
    lat_in = shift(lat_pair, "yl", 1)
    x_in = shift(x_own, "yl", 1)
    summed = scatter_x(scatter_z([recon_part[i * block:(i + 1) * block] for i in range(7)], far_low, far_high))
    recon_local = summed * SCALE_DEC + b_dec.reshape(D).astype(f32)
    err = (recon_local - x.astype(f32)).astype(bf16)
    recon = recon_local.astype(bf16).reshape(rows, 1, D)
    plane = gather_x(err)
    pieces, places = gather_z(jnp.concatenate([plane, shift(plane, "yl", 1)], axis=0))
    keep, send, lat_keep, half_dec, square = call(
        functools.partial(grad_kernel, places),
        [((half, nf), f32), ((half, nf), bf16), ((half, nf), bf16), ((nf, D), f32), ((nf, 1), f32)],
        [((tokens, D), bf16), ((tokens, nf), bf16), ((tokens, nf), f32)], 20,
        core, lat_own, lat_in, dec, *pieces)
    grad_part = keep + shift(send, "core", 1).astype(f32)
    square = square.reshape(nf)
    square = square + shift(square, "core", 1)
    square = square + shift(square, "yh", 1)
    grad = (grad_part + shift(grad_part.astype(bf16), "yh", 1).astype(f32)) * SCALE_DEC
    grad_pre = jnp.where(lat_keep > 0.0, grad, 0.0).astype(bf16)
    (new_enc,) = call(
        enc_kernel,
        [((D, nf), f32)],
        [((tokens, nf), bf16)], 20,
        core, grad_pre, shift(grad_pre, "core", 1), x_own, x_in, enc)
    row_rms = jnp.sqrt(square / (L * D) + EPSILON)
    factor = jnp.maximum(0.0, 1.0 - SHRINK_LEVEL / row_rms)
    new_dec = (half_dec * factor[:, None]).reshape(nf, 1, D)
    return recon, new_enc.reshape(1, D, nf), new_dec


def solution(mesh):
    fine = Mesh(mesh.devices.reshape(2, 2, 2, 8, 4), ("yh", "core", "yl", "z", "x"))
    layer, feat = ("yh", "core"), ("yl", "z", "x")
    return jax.shard_map(
        step,
        mesh=fine,
        in_specs=(P(feat, layer, None), P(layer, None, feat), P(feat), P(feat, layer, None), P(layer, None)),
        out_specs=(P(feat, layer, None), P(layer, None, feat), P(feat, layer, None)),
        check_vma=False,
    )
```

```python
import functools
import math

import jax
import jax.numpy as jnp
from jax import lax
from jax.experimental import pallas as pl
from jax.experimental.pallas import tpu as pltpu
from jax.sharding import Mesh, PartitionSpec as P


D = 2048
F = 16384
L = 4
SIZES = {"yh": 2, "core": 2, "yl": 2, "z": 8, "x": 4}
LEARN_RATE = 1.0
SHRINK_LEVEL = 0.5
EPSILON = 1e-06
SCALE_ENC = 1.0 / math.sqrt(L * D)
SCALE_DEC = 1.0 / math.sqrt(F)
LEAST = 2.0**-126
f32 = jnp.float32
bf16 = jnp.bfloat16


def shift(a, axis, k):
    n = SIZES[axis]
    return lax.ppermute(a, axis, [(i, (i + k) % n) for i in range(n)])


def gather_x(own):
    return jnp.concatenate([own, *(shift(own, "x", k) for k in (1, -1, 2))], axis=0)


def gather_z(plane):
    half = plane.shape[1] // 2
    pieces, places = [plane], [(0, 0)]
    down, up = plane, plane
    for i in range(3):
        down, up = shift(down, "z", 1), shift(up, "z", -1)
        pieces += [down, up]
        places += [(2 * i + 1, 0), (2 * i + 2, 0)]
        down, up = lax.optimization_barrier((down, up))
    pieces += [shift(down[:, :half], "z", 1), shift(up[:, half:], "z", -1)]
    places += [(7, 0), (7, half)]
    return pieces, tuple(places)


def scatter_z(blocks, far_low, far_high):
    home, down1, up1, down2, up2, down3, up3 = blocks
    half = far_low.shape[1]
    low, high = shift(far_low, "z", -1), shift(far_high, "z", 1)
    low, high = lax.optimization_barrier((low, high))
    low = jnp.concatenate([down3[:, :half] + low.astype(f32), down3[:, half:]], axis=1)
    high = jnp.concatenate([up3[:, :half], up3[:, half:] + high.astype(f32)], axis=1)
    for down, up in ((down2, up2), (down1, up1), (home, 0.0)):
        low, high = shift(low.astype(bf16), "z", -1), shift(high.astype(bf16), "z", 1)
        low, high = lax.optimization_barrier((low, high))
        low, high = down + low.astype(f32), up + high.astype(f32)
    return low + high


def rows_of(index, size):
    return pl.ds(pl.multiple_of(index * size, size), size)


def pre_kernel(places, enc_ref, enc2_ref, *refs):
    *pieces, x_own, keep, send, part = refs
    r = pieces[0].shape[0]
    for ref, (block, col) in zip(pieces, places):
        x_own[block * r:(block + 1) * r, col:col + ref.shape[1]] = ref[...]
    nf = enc_ref.shape[1]
    part[:, :nf] = jnp.dot(x_own[...], enc_ref[...], preferred_element_type=f32)
    part[:, nf:] = jnp.dot(x_own[...], enc2_ref[...], preferred_element_type=f32)
    core, half = lax.axis_index("core"), keep.shape[0]
    keep[...] = part[rows_of(core, half), :]
    send[...] = part[rows_of(1 - core, half), :]


def recon_kernel(mine_ref, other_ref, dec_ref, dec2_ref, lat_own, lat_pair, recon, far_low, far_high, latent):
    core, half = lax.axis_index("core"), mine_ref.shape[0]
    latent[rows_of(core, half), :] = mine_ref[...]
    latent[rows_of(1 - core, half), :] = other_ref[...]
    nf = dec_ref.shape[0]
    lat_own[...] = latent[:, :nf]
    lat_pair[...] = latent[:, nf:]
    recon[...] = jnp.dot(lat_own[...], dec_ref[...], preferred_element_type=f32)
    recon[...] += jnp.dot(lat_pair[...], dec2_ref[...], preferred_element_type=f32)
    r, cols = far_low.shape
    far_low[...] = recon[7 * r:, :cols].astype(bf16)
    far_high[...] = recon[7 * r:, cols:].astype(bf16)


def err_kernel(plane_ref, minus_ref, plus_ref, across_ref, x_ref, bias_ref, err, recon):
    order = (0, 3, 1, 2)
    rows = recon.shape[0]
    total = plane_ref[...].astype(f32)
    for ref, k in ((minus_ref, -1), (plus_ref, 1), (across_ref, 2)):
        got = ref[...].astype(f32)
        blocks = [order.index((o - k) % 4) for o in order]
        total += jnp.concatenate([got[i * rows:(i + 1) * rows, :] for i in blocks], axis=0)
    full = total * SCALE_DEC + bias_ref[...].astype(f32)
    err[...] = (full - x_ref[...].astype(f32)).astype(bf16)
    recon[...] = full[:rows, :].astype(bf16)


def join_kernel(own, other, both):
    r = own.shape[0]
    both[:r, :] = own[...]
    both[r:, :] = other[...]


def grad_kernel(places, lat_own, lat_in, dec_ref, *refs):
    *pieces, keep, send, lat_keep, half_dec, err_all, latent, part = refs
    r = pieces[0].shape[0] // 2
    half = lat_own.shape[0]
    for ref, (block, col) in zip(pieces, places):
        for pair in range(2):
            err_all[pair * half + block * r:pair * half + (block + 1) * r, col:col + ref.shape[1]] = ref[pair * r:(pair + 1) * r, :]
    latent[:half, :] = lat_own[...]
    latent[half:, :] = lat_in[...]
    part[...] = lax.dot_general(err_all[...], dec_ref[...], (((1,), (1,)), ((), ())), preferred_element_type=f32)
    grad = lax.dot_general(latent[...], err_all[...], (((0,), (0,)), ((), ())), preferred_element_type=f32)
    half_dec[...] = dec_ref[...].astype(f32) - grad * (LEARN_RATE * SCALE_DEC)
    square = jnp.sum(half_dec[...] * half_dec[...], axis=1, keepdims=True)
    extra = jnp.broadcast_to(square, (square.shape[0], 128)).T[:keep.shape[0] - half, :]
    core = lax.axis_index("core")
    keep[:half, :] = part[rows_of(core, half), :]
    keep[half:, :] = extra
    send[:half, :] = part[rows_of(1 - core, half), :].astype(bf16)
    send[half:, :] = extra.astype(bf16)
    lat_keep[...] = latent[rows_of(core, half), :]


def last_kernel(mine_ref, other_ref, square_ref, x_own, x_in, enc_ref, half_dec, new_enc, new_dec, grad):
    square = jnp.broadcast_to(square_ref[:1, :], (128, square_ref.shape[1])).T[:, :1]
    row_rms = jnp.sqrt(square / (L * D) + EPSILON)
    new_dec[...] = half_dec[...] * jnp.maximum(0.0, 1.0 - SHRINK_LEVEL / row_rms)
    core, half = lax.axis_index("core"), mine_ref.shape[0]
    grad[rows_of(core, half), :] = mine_ref[...]
    grad[rows_of(1 - core, half), :] = other_ref[...]
    dims = (((0,), (0,)), ((), ()))
    total = lax.dot_general(x_own[...], grad[:half, :], dims, preferred_element_type=f32)
    total += lax.dot_general(x_in[...], grad[half:, :], dims, preferred_element_type=f32)
    new_enc[...] = enc_ref[...].astype(f32) - total * (LEARN_RATE * SCALE_ENC)


def call(kernel, outs, scratch, mib, *args):
    vmem = pl.BlockSpec(memory_space=pltpu.VMEM)
    return pl.pallas_call(
        kernel,
        out_shape=[jax.ShapeDtypeStruct(s, d) for s, d in outs],
        in_specs=[vmem] * len(args),
        out_specs=[vmem] * len(outs),
        scratch_shapes=[pltpu.VMEM(s, d) for s, d in scratch],
        compiler_params=pltpu.CompilerParams(vmem_limit_bytes=mib * 1024 * 1024),
    )(*args)


def step(inputs, w_enc, b_enc, w_dec, b_dec):
    rows = inputs.shape[0]
    nf = w_enc.shape[2]
    tokens = rows * 64
    half, quarter, block = tokens // 2, tokens // 4, rows * 4
    x = inputs.reshape(rows, D)
    enc = w_enc.reshape(D, nf)
    dec = w_dec.reshape(nf, D)
    enc2, dec2 = shift(enc, "yl", 1), shift(dec, "yl", 1)
    bias = jnp.concatenate([b_enc, shift(b_enc, "yl", 1)]).astype(f32)

    x_plane = gather_x(x)
    pieces, places = gather_z(x_plane)
    x_own, keep, send = call(
        functools.partial(pre_kernel, places),
        [((half, D), bf16), ((quarter, 2 * nf), f32), ((quarter, 2 * nf), f32)],
        [((half, 2 * nf), f32)], 16,
        enc, enc2, *pieces)
    part = keep + shift(send, "core", 1)
    pre = (part + shift(part, "yh", 1)) * SCALE_ENC + bias
    latent = jnp.where(pre > 0.0, jnp.maximum(pre, LEAST), 0.0).astype(bf16)
    lat_own, lat_pair, recon_part, far_low, far_high = call(
        recon_kernel,
        [((half, nf), bf16), ((half, nf), bf16), ((half, D), f32), ((block, D // 2), bf16), ((block, D // 2), bf16)],
        [((half, 2 * nf), bf16)], 16,
        latent, shift(latent, "core", 1), dec, dec2)
    lat_in = shift(lat_pair, "yl", 1)
    x_in = shift(x_own, "yl", 1)
    plane = scatter_z([recon_part[i * block:(i + 1) * block] for i in range(7)], far_low, far_high).astype(bf16)
    err, recon = call(
        err_kernel,
        [((block, D), bf16), ((rows, D), bf16)], [], 8,
        plane, shift(plane, "x", 1), shift(plane, "x", -1), shift(plane, "x", 2), x_plane, b_dec)
    (both,) = call(join_kernel, [((2 * block, D), bf16)], [], 4, err, shift(err, "yl", 1))
    pieces, places = gather_z(both)
    keep, send, lat_keep, half_dec = call(
        functools.partial(grad_kernel, places),
        [((half + 16, nf), f32), ((half + 16, nf), bf16), ((half, nf), bf16), ((nf, D), f32)],
        [((tokens, D), bf16), ((tokens, nf), bf16), ((tokens, nf), f32)], 20,
        lat_own, lat_in, dec, *pieces)
    part = keep + shift(send, "core", 1).astype(f32)
    total = part + shift(part.astype(bf16), "yh", 1).astype(f32)
    grad_pre = jnp.where(lat_keep > 0.0, total[:half] * SCALE_DEC, 0.0).astype(bf16)
    new_enc, new_dec = call(
        last_kernel,
        [((D, nf), f32), ((nf, D), f32)],
        [((tokens, nf), bf16)], 24,
        grad_pre, shift(grad_pre, "core", 1), total[half:half + 8], x_own, x_in, enc, half_dec)
    return recon.reshape(rows, 1, D), new_enc.reshape(1, D, nf), new_dec.reshape(nf, 1, D)


def solution(mesh):
    fine = Mesh(mesh.devices.reshape(2, 2, 2, 8, 4), ("yh", "core", "yl", "z", "x"))
    layer, feat = ("yh", "core"), ("yl", "z", "x")
    return jax.shard_map(
        step,
        mesh=fine,
        in_specs=(P(feat, layer, None), P(layer, None, feat), P(feat), P(feat, layer, None), P(layer, None)),
        out_specs=(P(feat, layer, None), P(layer, None, feat), P(feat, layer, None)),
        check_vma=False,
    )
```

```python
import functools
import math

import jax
import jax.numpy as jnp
from jax import lax
from jax.experimental import pallas as pl
from jax.experimental.pallas import tpu as pltpu
from jax.sharding import Mesh, PartitionSpec as P


D = 2048
F = 16384
L = 4
SIZES = {"yh": 2, "core": 2, "yl": 2, "z": 8, "x": 4}
LEARN_RATE = 1.0
SHRINK_LEVEL = 0.5
EPSILON = 1e-06
STREAMS = 2
SCALE_ENC = 1.0 / math.sqrt(L * D)
SCALE_DEC = 1.0 / math.sqrt(F)
LEAST = 2.0**-126
f32 = jnp.float32
bf16 = jnp.bfloat16


def shift(a, axis, k):
    n = SIZES[axis]
    return lax.ppermute(a, axis, [(i, (i + k) % n) for i in range(n)])


def gather_x(own):
    return jnp.concatenate([own, *(shift(own, "x", k) for k in (1, -1, 2))], axis=0)


def gather_z(plane):
    half = plane.shape[1] // 2
    pieces, places = [plane], [(0, 0)]
    down, up = plane, plane
    for i in range(3):
        down, up = shift(down, "z", 1), shift(up, "z", -1)
        pieces += [down, up]
        places += [(2 * i + 1, 0), (2 * i + 2, 0)]
        down, up = lax.optimization_barrier((down, up))
    pieces += [shift(down[:, :half], "z", 1), shift(up[:, half:], "z", -1)]
    places += [(7, 0), (7, half)]
    return pieces, tuple(places)


def scatter_z(blocks, far_low, far_high):
    home, down1, up1, down2, up2, down3, up3 = blocks
    half = far_low.shape[1]
    low, high = shift(far_low, "z", -1), shift(far_high, "z", 1)
    low, high = lax.optimization_barrier((low, high))
    low = jnp.concatenate([down3[:, :half] + low.astype(f32), down3[:, half:]], axis=1)
    high = jnp.concatenate([up3[:, :half], up3[:, half:] + high.astype(f32)], axis=1)
    for down, up in ((down2, up2), (down1, up1), (home, 0.0)):
        low, high = shift(low.astype(bf16), "z", -1), shift(high.astype(bf16), "z", 1)
        low, high = lax.optimization_barrier((low, high))
        low, high = down + low.astype(f32), up + high.astype(f32)
    return low + high


def rows_of(index, size):
    return pl.ds(pl.multiple_of(index * size, size), size)


def pre_kernel(places, enc_ref, enc2_ref, *refs):
    *pieces, x_own, keep, send, bias, part = refs
    r = pieces[0].shape[0]
    for ref, (block, col) in zip(pieces, places):
        x_own[block * r:(block + 1) * r, col:col + ref.shape[1]] = ref[...]
    nf = enc_ref.shape[1]
    part[:, :nf] = jnp.dot(x_own[...], enc_ref[:D, :], preferred_element_type=f32)
    part[:, nf:] = jnp.dot(x_own[...], enc2_ref[:D, :], preferred_element_type=f32)
    bias[:, :nf] = enc_ref[D:D + 8, :].astype(f32)
    bias[:, nf:] = enc2_ref[D:D + 8, :].astype(f32)
    core, half = lax.axis_index("core"), keep.shape[0]
    keep[...] = part[rows_of(core, half), :]
    send[...] = part[rows_of(1 - core, half), :]


def recon_kernel(mine_ref, other_ref, dec_ref, dec2_ref, lat_own, lat_pair, recon, far_low, far_high, latent):
    core, half = lax.axis_index("core"), mine_ref.shape[0]
    latent[rows_of(core, half), :] = mine_ref[...]
    latent[rows_of(1 - core, half), :] = other_ref[...]
    nf = dec_ref.shape[0]
    lat_own[...] = latent[:, :nf]
    lat_pair[...] = latent[:, nf:]
    recon[...] = jnp.dot(lat_own[...], dec_ref[...], preferred_element_type=f32)
    recon[...] += jnp.dot(lat_pair[...], dec2_ref[...], preferred_element_type=f32)
    r, cols = far_low.shape
    far_low[...] = recon[7 * r:, :cols].astype(bf16)
    far_high[...] = recon[7 * r:, cols:].astype(bf16)


def err_kernel(plane_ref, minus_ref, plus_ref, across_ref, x_ref, bias_ref, err, recon):
    order = (0, 3, 1, 2)
    rows = recon.shape[0]
    total = plane_ref[...].astype(f32)
    for ref, k in ((minus_ref, -1), (plus_ref, 1), (across_ref, 2)):
        got = ref[...].astype(f32)
        blocks = [order.index((o - k) % 4) for o in order]
        total += jnp.concatenate([got[i * rows:(i + 1) * rows, :] for i in blocks], axis=0)
    full = total * SCALE_DEC + bias_ref[...].astype(f32)
    err[...] = (full - x_ref[...].astype(f32)).astype(bf16)
    recon[...] = full[:rows, :].astype(bf16)


def join_kernel(own, other, *streams):
    r, width = own.shape[0], streams[0].shape[1]
    for s, both in enumerate(streams):
        both[:r, :] = own[:, s * width:(s + 1) * width]
        both[r:, :] = other[:, s * width:(s + 1) * width]


def grad_kernel(places, lat_own, lat_in, dec_ref, *refs):
    *pieces, keep, send, lat_keep, half_dec, err_all, latent, part = refs
    r = pieces[0].shape[0] // 2
    half = lat_own.shape[0]
    for ref, (block, col) in zip(pieces, places):
        for pair in range(2):
            err_all[pair * half + block * r:pair * half + (block + 1) * r, col:col + ref.shape[1]] = ref[pair * r:(pair + 1) * r, :]
    latent[:half, :] = lat_own[...]
    latent[half:, :] = lat_in[...]
    part[...] = lax.dot_general(err_all[...], dec_ref[...], (((1,), (1,)), ((), ())), preferred_element_type=f32)
    grad = lax.dot_general(latent[...], err_all[...], (((0,), (0,)), ((), ())), preferred_element_type=f32)
    half_dec[...] = dec_ref[...].astype(f32) - grad * (LEARN_RATE * SCALE_DEC)
    square = jnp.sum(half_dec[...] * half_dec[...], axis=1, keepdims=True)
    extra = jnp.broadcast_to(square, (square.shape[0], 128)).T[:keep.shape[0] - half, :]
    core = lax.axis_index("core")
    keep[:half, :] = part[rows_of(core, half), :]
    keep[half:, :] = extra
    send[:half, :] = part[rows_of(1 - core, half), :].astype(bf16)
    send[half:, :] = extra.astype(bf16)
    lat_keep[...] = latent[rows_of(core, half), :]


def last_kernel(mine_ref, other_ref, square_ref, x_own, x_in, enc_ref, half_dec, new_enc, new_dec, grad, scaled, done):
    square = jnp.broadcast_to(square_ref[:1, :], (128, square_ref.shape[1])).T[:, :1]
    row_rms = jnp.sqrt(square / (L * D) + EPSILON)
    scaled[...] = half_dec[...] * jnp.maximum(0.0, 1.0 - SHRINK_LEVEL / row_rms)
    copy = pltpu.make_async_copy(scaled, new_dec.at[:, 0, :], done)
    copy.start()
    core, half = lax.axis_index("core"), mine_ref.shape[0]
    grad[rows_of(core, half), :] = mine_ref[...]
    grad[rows_of(1 - core, half), :] = other_ref[...]
    dims = (((0,), (0,)), ((), ()))
    total = lax.dot_general(x_own[...], grad[:half, :], dims, preferred_element_type=f32)
    total += lax.dot_general(x_in[...], grad[half:, :], dims, preferred_element_type=f32)
    new_enc[...] = enc_ref[...].astype(f32) - total * (LEARN_RATE * SCALE_ENC)
    copy.wait()


def call(kernel, outs, scratch, mib, *args):
    vmem = pl.BlockSpec(memory_space=pltpu.VMEM)
    return pl.pallas_call(
        kernel,
        out_shape=[jax.ShapeDtypeStruct(s, d) for s, d in outs],
        in_specs=[vmem] * len(args),
        out_specs=[vmem if len(s) == 2 else pl.BlockSpec(memory_space=pl.ANY) for s, _ in outs],
        scratch_shapes=[pltpu.VMEM(s, d) for s, d in scratch] + [pltpu.SemaphoreType.DMA] * any(len(s) == 3 for s, _ in outs),
        compiler_params=pltpu.CompilerParams(vmem_limit_bytes=mib * 1024 * 1024),
    )(*args)


def step(inputs, w_enc, b_enc, w_dec, b_dec):
    rows = inputs.shape[0]
    nf = w_enc.shape[2]
    tokens = rows * 64
    half, quarter, block = tokens // 2, tokens // 4, rows * 4
    x = inputs.reshape(rows, D)
    enc = w_enc.reshape(D, nf)
    dec = w_dec.reshape(nf, D)
    enc_bias = jnp.concatenate([enc, jnp.broadcast_to(b_enc, (16, nf))], axis=0)
    enc2, dec2 = shift(enc_bias, "yl", 1), shift(dec, "yl", 1)

    x_plane = gather_x(x)
    pieces, places = gather_z(x_plane)
    x_own, keep, send, bias = call(
        functools.partial(pre_kernel, places),
        [((half, D), bf16), ((quarter, 2 * nf), f32), ((quarter, 2 * nf), f32), ((8, 2 * nf), f32)],
        [((half, 2 * nf), f32)], 16,
        enc_bias, enc2, *pieces)
    part = keep + shift(send, "core", 1)
    pre = (part + shift(part, "yh", 1)) * SCALE_ENC + bias[:1]
    latent = jnp.where(pre > 0.0, jnp.maximum(pre, LEAST), 0.0).astype(bf16)
    lat_own, lat_pair, recon_part, far_low, far_high = call(
        recon_kernel,
        [((half, nf), bf16), ((half, nf), bf16), ((half, D), f32), ((block, D // 2), bf16), ((block, D // 2), bf16)],
        [((half, 2 * nf), bf16)], 16,
        latent, shift(latent, "core", 1), dec, dec2)
    lat_in = shift(lat_pair, "yl", 1)
    x_in = shift(x_own, "yl", 1)
    plane = scatter_z([recon_part[i * block:(i + 1) * block] for i in range(7)], far_low, far_high).astype(bf16)
    err, recon = call(
        err_kernel,
        [((block, D), bf16), ((rows, D), bf16)], [], 8,
        plane, shift(plane, "x", 1), shift(plane, "x", -1), shift(plane, "x", 2), x_plane, b_dec)
    width = D // STREAMS
    streams = call(join_kernel, [((2 * block, width), bf16)] * STREAMS, [], 4, err, shift(err, "yl", 1))
    pieces, places = [], []
    for s, both in enumerate(streams):
        got, where = gather_z(both)
        pieces += got
        places += [(b, c + s * width) for b, c in where]
    keep, send, lat_keep, half_dec = call(
        functools.partial(grad_kernel, places),
        [((half + 16, nf), f32), ((half + 16, nf), bf16), ((half, nf), bf16), ((nf, D), f32)],
        [((tokens, D), bf16), ((tokens, nf), bf16), ((tokens, nf), f32)], 20,
        lat_own, lat_in, dec, *pieces)
    part = keep + shift(send, "core", 1).astype(f32)
    total = part + shift(part.astype(bf16), "yh", 1).astype(f32)
    grad_pre = jnp.where(lat_keep > 0.0, total[:half] * SCALE_DEC, 0.0).astype(bf16)
    new_enc, new_dec = call(
        last_kernel,
        [((D, nf), f32), ((nf, 1, D), f32)],
        [((tokens, nf), bf16), ((nf, D), f32)], 24,
        grad_pre, shift(grad_pre, "core", 1), total[half:half + 8], x_own, x_in, enc, half_dec)
    return recon.reshape(rows, 1, D), new_enc.reshape(1, D, nf), new_dec


def solution(mesh):
    fine = Mesh(mesh.devices.reshape(2, 2, 2, 8, 4), ("yh", "core", "yl", "z", "x"))
    layer, feat = ("yh", "core"), ("yl", "z", "x")
    return jax.shard_map(
        step,
        mesh=fine,
        in_specs=(P(feat, layer, None), P(layer, None, feat), P(feat), P(feat, layer, None), P(layer, None)),
        out_specs=(P(feat, layer, None), P(layer, None, feat), P(feat, layer, None)),
        check_vma=False,
    )
```
